512 devices in a mesh: group: 128 (over y_hi, z, x), tensor: 4 (over y_lo, core).
Axes of the slice: x: 4, y: 4 (y_hi: 2, y_lo: 2; y = y_hi * 2 + y_lo), z: 16, core: 2. Of those that a mesh axis runs over, the one named last changes fastest.
Arguments:
- block: bfloat16 [128, 128, 1024], P('group'), may hold values from -6 to 6
- mask: int32 [128, 128], P('group'), may hold values 0 or 1
- cache_len: int32 [128], replicated, may hold values from 128 to 1920, as said below
- cache_k: bfloat16 [128, 1024, 1024], P('group', None, 'tensor'), may hold values from -240 to 240
- cache_v: bfloat16 [128, 1024, 1024], P('group', None, 'tensor'), may hold values from -6 to 6
- w_q: bfloat16 [1024, 1024], P(None, 'tensor'), may hold values from -0.1875 to 0.1875
- b_q: bfloat16 [1024], P('tensor'), may hold values from -3 to 3
- w_k: bfloat16 [1024, 1024], P(None, 'tensor'), may hold values from -0.1875 to 0.1875
- b_k: bfloat16 [1024], P('tensor'), may hold values from -3 to 3
- w_v: bfloat16 [1024, 1024], P(None, 'tensor'), may hold values from -0.1875 to 0.1875
- b_v: bfloat16 [1024], P('tensor'), may hold values from -3 to 3
- w_o: bfloat16 [1024, 1024], P('tensor'), may hold values from -0.1875 to 0.1875
- b_o: bfloat16 [1024], replicated, may hold values from -3 to 3
- ln_gain: bfloat16 [1024], replicated, may hold values from 0.5 to 1.5
- ln_shift: bfloat16 [1024], replicated, may hold values from -3 to 3
Outputs:
- denoised: bfloat16 [128, 128, 1024], P('group')
The draws below stay inside these ranges and needn't reach their ends.
Inputs may be any that keep to these rules, and one draw needn't show every extreme that they name: `cache_len`: in every pair exactly one request reads past its own group's slab into the partner's; the two lengths of a pair sum to at most 2048; both ends are reached in every draw.
All inputs are finite; a program needn't handle non-finite values. No bound on the sum of `mask` on one device may be relied on, other than what follows from the above.
Results may differ from the reference program's by a relative error of at most 0.03.
Values may be sent and summed in bfloat16 or wider, within the bound.
No kernel may reach another device: no remote copies, remote signals or barrier semaphores. Data moves between devices by JAX's collectives and lax.ppermute only.
A program may use at most 64 MiB of HBM per device.

```python
import jax
import jax.numpy as jnp
from jax import lax

D = 1024
HEADS = 16
HD = 64
BLK = 128
CACHE = 1024
GROUPS = 128


def draw_cache_len(key, part):
    pair_count = GROUPS // 2
    key_long = jax.random.fold_in(key, 11)
    key_short = jax.random.fold_in(key, 12)
    key_order = jax.random.fold_in(key, 13)
    top_len = 2 * CACHE - CACHE // 8
    long_len = jax.random.randint(key_long, (pair_count,), CACHE + 1, top_len + 1)
    long_len = long_len.at[0].set(top_len).at[pair_count - 1].set(top_len)
    spare_room = 2 * CACHE - long_len - CACHE // 8 + 1
    short_len = CACHE // 8 + jax.random.randint(key_short, (pair_count,), 0, 1 << 20) % spare_room
    short_len = short_len.at[0].set(CACHE // 8)
    long_first = jax.random.randint(key_order, (pair_count,), 0, 2)
    long_first = long_first.at[0].set(1).at[pair_count - 1].set(0)
    even_len = jnp.where(long_first == 1, long_len, short_len)
    odd_len = jnp.where(long_first == 1, short_len, long_len)
    return jnp.stack([even_len, odd_len], 1).reshape(GROUPS).astype(jnp.int32)


def draw_cache_k(key, part):
    normal_part = jnp.clip(jax.random.normal(key, (GROUPS, CACHE, D), jnp.float32), -6.0, 6.0)
    return normal_part.astype(jnp.bfloat16)


def plant(result, rng, low, high):
    place = [jax.random.randint(jax.random.fold_in(rng, axis), (), 0, length) for axis, length in enumerate(result.shape)]
    widest = result.shape.index(max(result.shape))
    neighbour = place[:widest] + [(place[widest] + 1) % result.shape[widest]] + place[widest + 1:]
    return result.at[tuple(place)].set(low).at[tuple(neighbour)].set(high)


def shard_levels(stream_key, shape, pieces, low, largest):
    level, own = 1.0, jax.random.fold_in(stream_key, 6)
    for dim, parts in pieces:
        draws = jnp.exp(jax.random.uniform(jax.random.fold_in(own, dim), (parts,), jnp.float32, low / len(pieces), largest / len(pieces)))
        level = level * jnp.repeat(draws, shape[dim] // parts).reshape([-1 if axis == dim else 1 for axis in range(len(shape))])
    return level


def noise(key, shape, width, most, shards=(), kind=jnp.bfloat16):
    result = jax.random.normal(key, shape, jnp.float32) * width
    if len(shards) > 0:
        result = shard_levels(key, shape, shards, -0.22, 0.18) * result
    return jnp.clip(result, min=-most, max=most).astype(kind)


def setup_inputs(seed: int = 0) -> dict:
    key_list = jax.random.split(jax.random.key(seed), 16)
    return {
        "block": noise(key_list[0], (GROUPS, BLK, D), 1.0, 6.0, ((0, 128),)),
        "mask": plant((jax.random.randint(key_list[1], (GROUPS, BLK), 0, 2) < 1).astype(jnp.int32), jax.random.fold_in(key_list[1], 1), 0, 1),
        "cache_len": draw_cache_len(jax.random.fold_in(key_list[15], 71), 0),
        "cache_k": draw_cache_k(jax.random.fold_in(key_list[15], 71), 0),
        "cache_v": noise(key_list[4], (GROUPS, CACHE, D), 1.0, 6.0, ((0, 128), (2, 4))),
        "w_q": noise(key_list[5], (D, D), D ** -0.5, 0.1875, ((1, 4),)),
        "b_q": noise(key_list[6], (D,), 0.5, 3.0, ((0, 4),)),
        "w_k": noise(key_list[7], (D, D), D ** -0.5, 0.1875, ((1, 4),)),
        "b_k": noise(key_list[8], (D,), 0.5, 3.0, ((0, 4),)),
        "w_v": noise(key_list[9], (D, D), D ** -0.5, 0.1875, ((1, 4),)),
        "b_v": noise(key_list[10], (D,), 0.5, 3.0, ((0, 4),)),
        "w_o": noise(key_list[11], (D, D), D ** -0.5, 0.1875, ((0, 4),)),
        "b_o": noise(key_list[12], (D,), 0.5, 3.0),
        "ln_gain": jnp.clip(1.0 + 0.1 * jax.random.normal(key_list[13], (D,), jnp.float32), 0.5, 1.5).astype(jnp.bfloat16),
        "ln_shift": noise(key_list[14], (D,), 0.5, 3.0),
    }


NEG = -1e+30
EPS = 1e-05

def project(inputs, weight, bias):
    return (jnp.dot(inputs, weight, preferred_element_type=jnp.float32) + bias.astype(jnp.float32)).astype(jnp.bfloat16)

def layer_norm(summed, ln_gain, ln_shift):
    centre = summed - lax.optimization_barrier(jnp.mean(summed, -1, keepdims=True))
    spread = lax.optimization_barrier(jnp.mean(centre * centre, -1, keepdims=True))
    return (centre * lax.rsqrt(spread + EPS) * ln_gain.astype(jnp.float32) + ln_shift.astype(jnp.float32)).astype(jnp.bfloat16)

def attend(queries, keys, values, usable):
    row_count = queries.shape[0]
    q_heads = queries.reshape(row_count, HEADS, HD).astype(jnp.float32)
    k_heads = keys.reshape(keys.shape[0], HEADS, HD).astype(jnp.float32)
    v_heads = values.reshape(values.shape[0], HEADS, HD).astype(jnp.float32)
    scores = jnp.einsum('qhd,khd->hqk', q_heads, k_heads) * HD ** (-0.5)
    scores = jnp.where(usable[None, None, :], scores, NEG)
    row_max = lax.optimization_barrier(jnp.max(scores, -1, keepdims=True))
    expo = jnp.exp(scores - row_max)
    row_sum = lax.optimization_barrier(jnp.sum(expo, -1))
    weights = lax.optimization_barrier(expo.astype(jnp.bfloat16)).astype(jnp.float32)
    summed_out = jnp.einsum('hqk,khd->qhd', weights, v_heads)
    return (summed_out / row_sum.T[:, :, None]).reshape(row_count, HEADS * HD).astype(jnp.bfloat16)

def reference(block, mask, cache_len, cache_k, cache_v, w_q, b_q, w_k, b_k, w_v, b_v, w_o, b_o, ln_gain, ln_shift):
    places = jnp.arange(2 * CACHE, dtype=jnp.int32)

    def one_group(group_idx):
        parity = group_idx % 2
        pair_base = (group_idx - parity).astype(jnp.int32)
        pool_k = lax.dynamic_slice_in_dim(cache_k, pair_base, 2, 0).reshape(2 * CACHE, D)
        pool_v = lax.dynamic_slice_in_dim(cache_v, pair_base, 2, 0).reshape(2 * CACHE, D)
        length = cache_len[group_idx]
        in_pool = jnp.where(parity == 0, places < length, places >= 2 * CACHE - length)
        usable = jnp.concatenate([in_pool, jnp.ones((BLK,), bool)], 0)
        tok_rows = block[group_idx]

        def one_pass(inputs):
            queries = project(inputs, w_q, b_q)
            new_k = project(inputs, w_k, b_k)
            new_v = project(inputs, w_v, b_v)
            attended = attend(queries, jnp.concatenate([pool_k, new_k], 0), jnp.concatenate([pool_v, new_v], 0), usable)
            summed = jnp.dot(attended, w_o, preferred_element_type=jnp.float32) + b_o.astype(jnp.float32) + inputs.astype(jnp.float32)
            return layer_norm(summed, ln_gain, ln_shift)
        first_out = one_pass(tok_rows)
        second = jnp.where(mask[group_idx][:, None] == 1, first_out, tok_rows)
        return one_pass(second)
    return lax.map(one_group, jnp.arange(GROUPS, dtype=jnp.int32))
```

```python
import jax
import jax.numpy as jnp
from jax import lax
from jax.experimental import pallas as pl
from jax.experimental.pallas import tpu as pltpu
from jax.sharding import PartitionSpec as P

HD = 64
NEG = -1e30
EPS = 1e-05
F32 = jnp.float32
BF16 = jnp.bfloat16
MIB = 1 << 20


def mm(left, right):
    return jnp.dot(left, right, preferred_element_type=F32)


def mm_t(left, right):
    return lax.dot_general(left, right, (((1,), (1,)), ((), ())), preferred_element_type=F32)


def project(rows, w_ref, b_ref):
    return (mm(rows, w_ref[...]) + b_ref[...].astype(F32)).astype(BF16)


def stack_heads(queries):
    scaled = queries * BF16(HD**-0.5)
    head_of = lax.broadcasted_iota(jnp.int32, scaled.shape, 1) // HD
    heads = scaled.shape[1] // HD
    return jnp.concatenate(
        [jnp.where(head_of == head, scaled, jnp.zeros_like(scaled)) for head in range(heads)], 0
    )


def unstack_heads(stacked, rows):
    heads = stacked.shape[0] // rows
    head_of = lax.broadcasted_iota(jnp.int32, (rows, stacked.shape[1]), 1) // HD
    merged = stacked[:rows]
    for head in range(1, heads):
        merged = jnp.where(head_of == head, stacked[head * rows : (head + 1) * rows], merged)
    return merged


def bias_row(count, low, high):
    place = lax.broadcasted_iota(jnp.int32, (1, count), 1)
    return jnp.where((place >= low) & (place < high), F32(0), F32(NEG))


def layer_norm(summed, gain_ref, shift_ref):
    centre = summed - jnp.mean(summed, -1, keepdims=True)
    spread = jnp.mean(centre * centre, -1, keepdims=True)
    return (
        centre * lax.rsqrt(spread + EPS) * gain_ref[...].astype(F32) + shift_ref[...].astype(F32)
    ).astype(BF16)


def own_kernel(
    lim_ref, x_ref, wq_ref, wk_ref, wv_ref, bq_ref, bk_ref, bv_ref, k_ref, v_ref,
    q_ref, acc_ref, max_ref, sum_ref,
):
    rows = x_ref[...]
    stacked = stack_heads(project(rows, wq_ref, bq_ref))
    q_ref[...] = stacked
    new_k = project(rows, wk_ref, bk_ref)
    new_v = project(rows, wv_ref, bv_ref)
    s_own = mm_t(stacked, k_ref[...]) + bias_row(k_ref.shape[0], lim_ref[0], lim_ref[1])
    s_new = mm_t(stacked, new_k)
    top = jnp.maximum(jnp.max(s_own, -1, keepdims=True), jnp.max(s_new, -1, keepdims=True))
    e_own = jnp.exp(s_own - top)
    e_new = jnp.exp(s_new - top)
    total = jnp.sum(e_own, -1, keepdims=True) + jnp.sum(e_new, -1, keepdims=True)
    acc_ref[...] = mm(e_own.astype(BF16), v_ref[...]) + mm(e_new.astype(BF16), new_v)
    max_ref[...] = jnp.broadcast_to(top, max_ref.shape)
    sum_ref[...] = jnp.broadcast_to(total, sum_ref.shape)


def peer_score_kernel(lim_ref, q_ref, k_ref, acc_ref, max_ref, sum_ref, e_ref, out_ref, total_ref):
    scores = mm_t(q_ref[...], k_ref[...]) + bias_row(k_ref.shape[0], lim_ref[2], lim_ref[3])
    before = max_ref[:, :1]
    top = jnp.maximum(before, jnp.max(scores, -1, keepdims=True))
    expo = jnp.exp(scores - top)
    shrink = jnp.exp(before - top)
    total = sum_ref[:, :1] * shrink + jnp.sum(expo, -1, keepdims=True)
    e_ref[...] = expo.astype(BF16)
    out_ref[...] = acc_ref[...] * shrink
    total_ref[...] = jnp.broadcast_to(total, total_ref.shape)


def peer_value_kernel(e_ref, v_ref, acc_ref, total_ref, att_ref):
    summed = acc_ref[...] + mm(e_ref[...], v_ref[...])
    att_ref[...] = unstack_heads(summed / total_ref[:, :1], att_ref.shape[0]).astype(BF16)


def out_project(lim_ref, att_ref, wo_refs, bo_ref, rows, gain_ref, shift_ref):
    summed = bo_ref[...].astype(F32) + rows.astype(F32)
    me = lim_ref[4]
    for apart, wo_ref in enumerate(wo_refs):
        summed += mm(att_ref[me ^ apart], wo_ref[...])
    return layer_norm(summed, gain_ref, shift_ref)


def second_kernel(
    lim_ref, att_ref, wo0, wo1, wo2, wo3, bo_ref, gain_ref, shift_ref, x_ref, mask_ref,
    wq_ref, wk_ref, wv_ref, bq_ref, bk_ref, bv_ref, k_ref, v_ref, pk_ref, pv_ref,
    second_ref, att_out_ref,
):
    block = x_ref[...]
    first = out_project(lim_ref, att_ref, (wo0, wo1, wo2, wo3), bo_ref, block, gain_ref, shift_ref)
    rows = jnp.where(mask_ref[:, :1] == 1, first, block)
    second_ref[...] = rows
    stacked = stack_heads(project(rows, wq_ref, bq_ref))
    new_k = project(rows, wk_ref, bk_ref)
    new_v = project(rows, wv_ref, bv_ref)
    count = k_ref.shape[0]
    s_own = mm_t(stacked, k_ref[...]) + bias_row(count, lim_ref[0], lim_ref[1])
    s_peer = mm_t(stacked, pk_ref[...]) + bias_row(count, lim_ref[2], lim_ref[3])
    s_new = mm_t(stacked, new_k)
    top = jnp.maximum(
        jnp.maximum(jnp.max(s_own, -1, keepdims=True), jnp.max(s_peer, -1, keepdims=True)),
        jnp.max(s_new, -1, keepdims=True),
    )
    e_own = jnp.exp(s_own - top)
    e_peer = jnp.exp(s_peer - top)
    e_new = jnp.exp(s_new - top)
    total = (
        jnp.sum(e_own, -1, keepdims=True)
        + jnp.sum(e_peer, -1, keepdims=True)
        + jnp.sum(e_new, -1, keepdims=True)
    )
    summed = (
        mm(e_own.astype(BF16), v_ref[...])
        + mm(e_peer.astype(BF16), pv_ref[...])
        + mm(e_new.astype(BF16), new_v)
    )
    att_out_ref[...] = unstack_heads(summed / total, block.shape[0]).astype(BF16)


def last_kernel(lim_ref, att_ref, wo0, wo1, wo2, wo3, bo_ref, gain_ref, shift_ref, x_ref, out_ref):
    out_ref[...] = out_project(
        lim_ref, att_ref, (wo0, wo1, wo2, wo3), bo_ref, x_ref[...], gain_ref, shift_ref
    )


def call(kernel, name, outs, *args, flops=1 << 28, limit=24):
    specs = [pl.BlockSpec(memory_space=pltpu.SMEM) if arg.ndim == 1 else pl.BlockSpec(memory_space=pltpu.VMEM) for arg in args]
    return pl.pallas_call(
        kernel,
        name=name,
        out_shape=outs,
        in_specs=specs,
        out_specs=jax.tree.map(lambda _: pl.BlockSpec(memory_space=pltpu.VMEM), outs),
        compiler_params=pltpu.CompilerParams(vmem_limit_bytes=limit * MIB),
        cost_estimate=pl.CostEstimate(flops=flops, bytes_accessed=1 << 22, transcendentals=1 << 19),
    )(*args)


def moved(array, axis, apart):
    return lax.ppermute(array, axis, [(i, i ^ apart) for i in range(lax.axis_size(axis))])


def body(
    block, mask, cache_len, cache_k, cache_v, w_q, b_q, w_k, b_k, w_v, b_v, w_o, b_o, ln_gain, ln_shift
):
    rows = block[0]
    own_k, own_v = cache_k[0], cache_v[0]
    slab, width = own_k.shape
    count = rows.shape[0]
    stack = count * (width // HD)
    group = lax.axis_index("group")
    parity = group % 2
    length = cache_len[group]
    even = parity == 0
    lims = jnp.stack(
        [
            jnp.where(even, 0, slab - length),
            jnp.where(even, length, slab),
            jnp.where(even, 0, 2 * slab - length),
            jnp.where(even, length - slab, slab),
            lax.axis_index("tensor"),
        ]
    ).astype(jnp.int32)
    row = lambda vector: vector.reshape(1, -1)
    b_q, b_k, b_v, b_o, ln_gain, ln_shift = map(row, (b_q, b_k, b_v, b_o, ln_gain, ln_shift))
    mask_cols = jnp.broadcast_to(mask[0][:, None], (count, 128))

    peer_k = moved(own_k, "group", 1)
    peer_v = moved(own_v, "group", 1)
    wo_late, lims = lax.optimization_barrier((w_o, lims))
    wo2 = moved(wo_late, "tensor", 2)
    shape = jax.ShapeDtypeStruct
    stats = shape((stack, 128), F32)
    q_stack, acc, top, total = call(
        own_kernel, "own",
        (shape((stack, width), BF16), shape((stack, width), F32), stats, stats),
        lims, rows, w_q, w_k, w_v, b_q, b_k, b_v, own_k, own_v,
    )
    wo_later, acc = lax.optimization_barrier((w_o, acc))
    wo1 = moved(wo_later, "tensor", 1)
    wo2, acc = lax.optimization_barrier((wo2, acc))
    wo3 = moved(wo2, "tensor", 1)
    wo = (w_o, wo1, wo2, wo3)
    expo, acc, total = call(
        peer_score_kernel, "peer_score",
        (shape((stack, slab), BF16), shape((stack, width), F32), stats),
        lims, q_stack, peer_k, acc, top, total,
    )
    att = call(peer_value_kernel, "peer_value", shape((count, width), BF16), expo, peer_v, acc, total)
    att = lax.all_gather(att, "tensor")
    second, att = call(
        second_kernel, "second",
        (shape(rows.shape, BF16), shape((count, width), BF16)),
        lims, att, *wo, b_o, ln_gain, ln_shift, rows, mask_cols,
        w_q, w_k, w_v, b_q, b_k, b_v, own_k, own_v, peer_k, peer_v,
    )
    att = lax.all_gather(att, "tensor")
    out = call(
        last_kernel, "last", shape(rows.shape, BF16),
        lims, att, *wo, b_o, ln_gain, ln_shift, second,
    )
    return out[None]


def solution(mesh):
    return jax.shard_map(
        body,
        mesh=mesh,
        in_specs=(
            P("group", None, None),
            P("group", None),
            P(),
            P("group", None, "tensor"),
            P("group", None, "tensor"),
            P(None, "tensor"),
            P("tensor"),
            P(None, "tensor"),
            P("tensor"),
            P(None, "tensor"),
            P("tensor"),
            P("tensor", None),
            P(),
            P(),
            P(),
        ),
        out_specs=P("group", None, None),
        check_vma=False,
    )
```

```python
import jax
import jax.numpy as jnp
from jax import lax
from jax.experimental import pallas as pl
from jax.experimental.pallas import tpu as pltpu
from jax.sharding import PartitionSpec as P

HD = 64
SHORTEST = 128
NEG = -1e30
EPS = 1e-05
F32 = jnp.float32
BF16 = jnp.bfloat16
MIB = 1 << 20
LOG2E = 1.4426950408889634
STEP = 16


def mm(left, right):
    return jnp.dot(left, right, preferred_element_type=F32)


def mm_t(left, right):
    return lax.dot_general(left, right, (((1,), (1,)), ((), ())), preferred_element_type=F32)


def project(rows, w_ref, b_ref):
    return (mm(rows, w_ref[...]) + b_ref[...].astype(F32)[None]).astype(BF16)


def stack_queries(rows, w_ref, b_ref):
    scaled = (
        (mm(rows, w_ref[...]) + b_ref[...].astype(F32)[None]) * F32(LOG2E * HD**-0.5)
    ).astype(BF16)
    head_of = lax.broadcasted_iota(jnp.int32, scaled.shape, 1) // HD
    heads = scaled.shape[1] // HD
    return jnp.concatenate(
        [jnp.where(head_of == head, scaled, jnp.zeros_like(scaled)) for head in range(heads)], 0
    )


def unstack_heads(stacked, rows):
    heads = stacked.shape[0] // rows
    head_of = lax.broadcasted_iota(jnp.int32, (rows, stacked.shape[1]), 1) // HD
    merged = stacked[:rows]
    for head in range(1, heads):
        merged = jnp.where(head_of == head, stacked[head * rows : (head + 1) * rows], merged)
    return merged


def own_span(len_ref, slab):
    group = lax.axis_index("group")
    length = len_ref[group]
    even = group % 2 == 0
    return jnp.where(even, 0, slab - length), jnp.where(even, length, slab)


def peer_span(len_ref, kept):
    group = lax.axis_index("group")
    beyond = len_ref[group] - (kept + SHORTEST)
    even = group % 2 == 0
    return jnp.where(even, 0, kept - beyond), jnp.where(even, beyond, kept)


def bias_row(count, span):
    low, high = span
    place = lax.broadcasted_iota(jnp.int32, (1, count), 1)
    return jnp.where((place >= low) & (place < high), F32(0), F32(NEG))


def column(row_ref):
    count = row_ref.shape[1]
    square = jnp.broadcast_to(row_ref[...], (count, count))
    across = lax.broadcasted_iota(jnp.int32, square.shape, 1)
    down = lax.broadcasted_iota(jnp.int32, square.shape, 0)
    return jnp.sum(jnp.where(across == down, square, 0), -1, keepdims=True)


def layer_norm(summed, norm_ref):
    centre = summed - jnp.mean(summed, -1, keepdims=True)
    spread = jnp.mean(centre * centre, -1, keepdims=True)
    return (
        centre * lax.rsqrt(spread + EPS) * norm_ref[1:2, :] + norm_ref[2:3, :]
    ).astype(BF16)


def own_kernel(
    len_ref, mask_ref, x_ref, wq_ref, wk_ref, wv_ref, bq_ref, bk_ref, bv_ref, k_ref, v_ref,
    bo_ref, gain_ref, shift_ref,
    q_ref, acc_ref, max_ref, sum_ref, picked_ref, norm_ref, bias_ref, kt_ref,
):
    slab = k_ref.shape[0]
    picked_ref[...] = jnp.broadcast_to(column(mask_ref), picked_ref.shape)
    for place, vector_ref in enumerate((bo_ref, gain_ref, shift_ref)):
        norm_ref[place : place + 1, :] = vector_ref[...].astype(F32)[None]
    own_bias = bias_row(slab, own_span(len_ref, slab))
    bias_ref[:, :slab] = jnp.broadcast_to(own_bias, (bias_ref.shape[0], slab))
    kept = slab - SHORTEST
    bias_ref[:, slab:] = jnp.broadcast_to(
        bias_row(kept, peer_span(len_ref, kept)), (bias_ref.shape[0], kept)
    )
    rows = x_ref[...]
    stacked = stack_queries(rows, wq_ref, bq_ref)
    q_ref[...] = stacked
    new_k = project(rows, wk_ref, bk_ref)
    new_v = project(rows, wv_ref, bv_ref)
    kt_ref[...] = k_ref[...].T
    s_own = mm(stacked, kt_ref[...]) + own_bias
    s_new = mm_t(stacked, new_k)
    top = jnp.maximum(jnp.max(s_own, -1, keepdims=True), jnp.max(s_new, -1, keepdims=True))
    e_own = jnp.exp2(s_own - top)
    e_new = jnp.exp2(s_new - top)
    total = jnp.sum(e_own, -1, keepdims=True) + jnp.sum(e_new, -1, keepdims=True)
    acc_ref[...] = mm(e_own.astype(BF16), v_ref[...]) + mm(e_new.astype(BF16), new_v)
    max_ref[...] = jnp.broadcast_to(top, max_ref.shape)
    sum_ref[...] = jnp.broadcast_to(total, sum_ref.shape)


def send_kernel(slab_hbm, out_ref, sem):
    kept = out_ref.shape[0]
    first = pl.multiple_of(
        jnp.where(lax.axis_index("group") % 2 == 0, slab_hbm.shape[0] - kept, 0), SHORTEST
    )
    load = pltpu.make_async_copy(slab_hbm.at[pl.ds(first, kept)], out_ref, sem)
    load.start()
    load.wait()


def peer_score_kernel(
    bias_ref, q_ref, k_ref, acc_ref, max_ref, sum_ref, e_ref, out_ref, total_ref, kt_ref
):
    kept = k_ref.shape[0]
    kt_ref[...] = k_ref[...].T
    scores = mm(q_ref[...], kt_ref[...]) + bias_ref[0:1, bias_ref.shape[1] - kept :]
    before = max_ref[:, :1]
    top = jnp.maximum(before, jnp.max(scores, -1, keepdims=True))
    expo = jnp.exp2(scores - top)
    shrink = jnp.exp2(before - top)
    total = sum_ref[:, :1] * shrink + jnp.sum(expo, -1, keepdims=True)
    e_ref[...] = expo.astype(BF16)
    out_ref[...] = acc_ref[...] * shrink
    total_ref[...] = jnp.broadcast_to(total, total_ref.shape)


def peer_value_kernel(e_ref, v_ref, acc_ref, total_ref, att_ref):
    summed = acc_ref[...] + mm(e_ref[...], v_ref[...])
    att_ref[...] = unstack_heads(summed / total_ref[:, :1], att_ref.shape[0]).astype(BF16)


def out_project(att_ref, wo_refs, rows, norm_ref):
    summed = norm_ref[0:1, :] + rows.astype(F32)
    me = lax.axis_index("tensor")
    for apart, wo_ref in enumerate(wo_refs):
        summed += mm(att_ref[me ^ apart], wo_ref[...])
    return layer_norm(summed, norm_ref)


def second_kernel(
    bias_ref, att_ref, wo0, wo1, wo2, wo3, norm_ref, x_ref, picked_ref,
    wq_ref, wk_ref, wv_ref, bq_ref, bk_ref, bv_ref, kt_ref, v_ref, pkt_ref, pv_ref,
    second_ref, att_out_ref, s_ref, e_ref,
):
    block = x_ref[...]
    first = out_project(att_ref, (wo0, wo1, wo2, wo3), block, norm_ref)
    rows = jnp.where(picked_ref[:, :1] == 1, first, block)
    second_ref[...] = rows
    stacked = stack_queries(rows, wq_ref, bq_ref)
    own, cached = kt_ref.shape[1], kt_ref.shape[1] + pkt_ref.shape[1]
    s_ref[:, :own] = mm(stacked, kt_ref[...])
    s_ref[:, own:cached] = mm(stacked, pkt_ref[...])
    new_k = project(rows, wk_ref, bk_ref)
    new_v = project(rows, wv_ref, bv_ref)
    s_ref[:, cached:] = mm_t(stacked, new_k)
    bias = bias_ref[0:1, :]
    count = rows.shape[0]
    head_of = lax.broadcasted_iota(jnp.int32, att_out_ref.shape, 1) // HD
    merged = jnp.zeros(att_out_ref.shape, F32)
    for head in range(stacked.shape[0] // count):
        sums = []
        for low in range(head * count, (head + 1) * count, STEP):
            at = slice(low, low + STEP)
            s_old = s_ref[at, :cached] + bias
            s_new = s_ref[at, cached:]
            top = jnp.maximum(jnp.max(s_old, -1, keepdims=True), jnp.max(s_new, -1, keepdims=True))
            e_old = jnp.exp2(s_old - top)
            e_new = jnp.exp2(s_new - top)
            sums.append(jnp.sum(e_old, -1, keepdims=True) + jnp.sum(e_new, -1, keepdims=True))
            e_ref[at, :cached] = e_old.astype(BF16)
            e_ref[at, cached:] = e_new.astype(BF16)
        at = slice(head * count, (head + 1) * count)
        summed = (
            mm(e_ref[at, :own], v_ref[...])
            + mm(e_ref[at, own:cached], pv_ref[...])
            + mm(e_ref[at, cached:], new_v)
        ) / jnp.concatenate(sums, 0)
        merged = jnp.where(head_of == head, summed, merged)
    att_out_ref[...] = merged.astype(BF16)


def last_kernel(att_ref, wo0, wo1, wo2, wo3, norm_ref, x_ref, out_ref):
    out_ref[...] = out_project(
        att_ref, (wo0, wo1, wo2, wo3), x_ref[...], norm_ref
    )


def call(kernel, name, outs, *args, in_hbm=(), scratch=(), flops=1 << 10, limit=24):
    specs = [
        pl.BlockSpec(memory_space=pltpu.SMEM if arg.dtype == jnp.int32 and arg.ndim == 1 else pltpu.VMEM)
        for arg in args
    ] + [pl.BlockSpec(memory_space=pltpu.HBM)] * len(in_hbm)
    return pl.pallas_call(
        kernel,
        name=name,
        out_shape=outs,
        in_specs=specs,
        out_specs=jax.tree.map(lambda _: pl.BlockSpec(memory_space=pltpu.VMEM), outs),
        scratch_shapes=scratch,
        compiler_params=pltpu.CompilerParams(vmem_limit_bytes=limit * MIB),
        cost_estimate=pl.CostEstimate(flops=flops, bytes_accessed=1 << 10, transcendentals=0),
    )(*args, *in_hbm)


def after(array, other):
    return lax.optimization_barrier((array, other))[0]


def moved(array, axis, apart):
    return lax.ppermute(array, axis, [(i, i ^ apart) for i in range(lax.axis_size(axis))])


def body(
    block, mask, cache_len, cache_k, cache_v, w_q, b_q, w_k, b_k, w_v, b_v, w_o, b_o, ln_gain, ln_shift
):
    rows = block[0]
    own_k, own_v = cache_k[0], cache_v[0]
    slab, width = own_k.shape
    count = rows.shape[0]
    stack = count * (width // HD)

    shape = jax.ShapeDtypeStruct
    dma = pltpu.SemaphoreType.DMA

    def sendable(array, name):
        return call(
            send_kernel, name, shape((slab - SHORTEST, width), BF16), in_hbm=(array,), scratch=[dma]
        )

    send_k = sendable(own_k, "send_k")
    send_v = sendable(after(own_v, send_k), "send_v")
    peer_k = moved(send_k, "group", 1)
    peer_v = moved(send_v, "group", 1)
    wo2 = moved(w_o, "tensor", 2)
    stats = shape((stack, 128), F32)
    q_stack, acc, top, total, picked, norm, bias, own_kt = call(
        own_kernel, "own",
        (shape((stack, width), BF16), shape((stack, width), F32), stats, stats, shape((count, 128), jnp.int32), shape((8, rows.shape[1]), F32),
         shape((8, 2 * slab - SHORTEST), F32), shape((width, slab), BF16)),
        cache_len, mask, rows, w_q, w_k, w_v, b_q, b_k, b_v, own_k, own_v,
        b_o, ln_gain, ln_shift,
    )
    wo1 = moved(after(w_o, acc), "tensor", 1)
    expo, acc, total, peer_kt = call(
        peer_score_kernel, "peer_score",
        (shape((stack, slab - SHORTEST), BF16), shape((stack, width), F32), stats,
         shape((width, slab - SHORTEST), BF16)),
        bias, q_stack, peer_k, acc, top, total, flops=1 << 33,
    )
    wo3 = moved(after(wo2, expo), "tensor", 1)
    wo = (w_o, wo1, wo2, wo3)
    att = call(peer_value_kernel, "peer_value", shape((count, width), BF16), expo, peer_v, acc, total)
    att = lax.all_gather(att, "tensor")
    second, att = call(
        second_kernel, "second",
        (shape(rows.shape, BF16), shape((count, width), BF16)),
        bias, att, *wo, norm, rows, picked,
        w_q, w_k, w_v, b_q, b_k, b_v, own_kt, own_v, peer_kt, peer_v,
        scratch=[pltpu.VMEM((stack, 2 * slab), F32), pltpu.VMEM((stack, 2 * slab), BF16)],
    )
    att = lax.all_gather(att, "tensor")
    out = call(
        last_kernel, "last", shape(rows.shape, BF16),
        att, *wo, norm, second,
    )
    return out[None]


def solution(mesh):
    return jax.shard_map(
        body,
        mesh=mesh,
        in_specs=(
            P("group", None, None),
            P("group", None),
            P(),
            P("group", None, "tensor"),
            P("group", None, "tensor"),
            P(None, "tensor"),
            P("tensor"),
            P(None, "tensor"),
            P("tensor"),
            P(None, "tensor"),
            P("tensor"),
            P("tensor", None),
            P(),
            P(),
            P(),
        ),
        out_specs=P("group", None, None),
        check_vma=False,
    )
```

```python
import jax
import jax.numpy as jnp
from jax import lax
from jax.experimental import pallas as pl
from jax.experimental.pallas import tpu as pltpu
from jax.sharding import PartitionSpec as P

HD = 64
SHORTEST = 128
NEG = -1e30
EPS = 1e-05
F32 = jnp.float32
BF16 = jnp.bfloat16
MIB = 1 << 20
LOG2E = 1.4426950408889634
STEP = 16


def mm(left, right):
    return jnp.dot(left, right, preferred_element_type=F32)


def mm_t(left, right):
    return lax.dot_general(left, right, (((1,), (1,)), ((), ())), preferred_element_type=F32)


def project(rows, w_ref, b_ref):
    return (mm(rows, w_ref[...]) + b_ref[...].astype(F32)[None]).astype(BF16)


def stack_queries(rows, w_ref, b_ref):
    scaled = (
        (mm(rows, w_ref[...]) + b_ref[...].astype(F32)[None]) * F32(LOG2E * HD**-0.5)
    ).astype(BF16)
    head_of = lax.broadcasted_iota(jnp.int32, scaled.shape, 1) // HD
    heads = scaled.shape[1] // HD
    return jnp.concatenate(
        [jnp.where(head_of == head, scaled, jnp.zeros_like(scaled)) for head in range(heads)], 0
    )


def unstack_heads(stacked, rows):
    heads = stacked.shape[0] // rows
    head_of = lax.broadcasted_iota(jnp.int32, (rows, stacked.shape[1]), 1) // HD
    merged = stacked[:rows]
    for head in range(1, heads):
        merged = jnp.where(head_of == head, stacked[head * rows : (head + 1) * rows], merged)
    return merged


def read_length(len_ref):
    group = lax.axis_index("group")
    place = lax.broadcasted_iota(jnp.int32, len_ref.shape, 1)
    return jnp.sum(jnp.where(place == group, len_ref[...], 0), -1, keepdims=True)


def own_span(length, slab):
    even = lax.axis_index("group") % 2 == 0
    return jnp.where(even, 0, slab - length), jnp.where(even, length, slab)


def peer_span(length, kept):
    beyond = length - (kept + SHORTEST)
    even = lax.axis_index("group") % 2 == 0
    return jnp.where(even, 0, kept - beyond), jnp.where(even, beyond, kept)


def bias_row(count, span):
    low, high = span
    place = lax.broadcasted_iota(jnp.int32, (1, count), 1)
    return jnp.where((place >= low) & (place < high), F32(0), F32(NEG))


def column(row_ref):
    count = row_ref.shape[1]
    square = jnp.broadcast_to(row_ref[...], (count, count))
    across = lax.broadcasted_iota(jnp.int32, square.shape, 1)
    down = lax.broadcasted_iota(jnp.int32, square.shape, 0)
    return jnp.sum(jnp.where(across == down, square, 0), -1, keepdims=True)


def layer_norm(summed, norm_ref):
    centre = summed - jnp.mean(summed, -1, keepdims=True)
    spread = jnp.mean(centre * centre, -1, keepdims=True)
    return (centre * lax.rsqrt(spread + EPS) * norm_ref[1:2, :] + norm_ref[2:3, :]).astype(BF16)


def chunks(low, high, step):
    return [slice(start, start + step) for start in range(low, high, step)]


def own_kernel(
    len_ref, mask_ref, x_ref, wq_ref, wk_ref, wv_ref, bq_ref, bk_ref, bv_ref, k_ref, v_ref,
    bo_ref, gain_ref, shift_ref,
    q_ref, acc_ref, stat_ref, picked_ref, norm_ref, bias_ref, kt_ref, s_ref, e_ref,
):
    slab, count = k_ref.shape[0], x_ref.shape[0]
    rows = x_ref[...]
    stacked = stack_queries(rows, wq_ref, bq_ref)
    q_ref[...] = stacked
    kt_ref[...] = k_ref[...].T
    s_ref[:, :slab] = mm(stacked, kt_ref[...])
    new_k = project(rows, wk_ref, bk_ref)
    new_v = project(rows, wv_ref, bv_ref)
    s_ref[:, slab:] = mm_t(stacked, new_k)
    length = read_length(len_ref)
    own_bias = bias_row(slab, own_span(length, slab))
    bias_ref[:, :slab] = jnp.broadcast_to(own_bias, (bias_ref.shape[0], slab))
    kept = slab - SHORTEST
    bias_ref[:, slab:] = jnp.broadcast_to(
        bias_row(kept, peer_span(length, kept)), (bias_ref.shape[0], kept)
    )
    picked_ref[...] = jnp.broadcast_to(column(mask_ref), picked_ref.shape)
    for place, vector_ref in enumerate((bo_ref, gain_ref, shift_ref)):
        norm_ref[place : place + 1, :] = vector_ref[...].astype(F32)[None]
    bias = bias_ref[0:1, :slab]
    half = stat_ref.shape[1] // 2
    for block in chunks(0, stacked.shape[0], count):
        for at in chunks(block.start, block.stop, STEP):
            s_old = s_ref[at, :slab] + bias
            s_new = s_ref[at, slab:]
            top = jnp.maximum(jnp.max(s_old, -1, keepdims=True), jnp.max(s_new, -1, keepdims=True))
            e_old = jnp.exp2(s_old - top)
            e_new = jnp.exp2(s_new - top)
            total = jnp.sum(e_old, -1, keepdims=True) + jnp.sum(e_new, -1, keepdims=True)
            e_ref[at, :slab] = e_old.astype(BF16)
            e_ref[at, slab:] = e_new.astype(BF16)
            stat_ref[at, :half] = jnp.broadcast_to(top, (STEP, half))
            stat_ref[at, half:] = jnp.broadcast_to(total, (STEP, half))
        acc_ref[block, :] = mm(e_ref[block, :slab], v_ref[...]) + mm(e_ref[block, slab:], new_v)


def send_kernel(slab_hbm, out_ref, sem):
    kept = out_ref.shape[0]
    first = pl.multiple_of(
        jnp.where(lax.axis_index("group") % 2 == 0, slab_hbm.shape[0] - kept, 0), SHORTEST
    )
    load = pltpu.make_async_copy(slab_hbm.at[pl.ds(first, kept)], out_ref, sem)
    load.start()
    load.wait()


def peer_score_kernel(
    bias_ref, q_ref, k_ref, acc_ref, stat_ref, e_ref, out_ref, scale_ref, kt_ref, s_ref, peer_ref
):
    kept = k_ref.shape[0]
    half = stat_ref.shape[1] // 2
    kt_ref[...] = k_ref[...].T
    bias = bias_ref[0:1, bias_ref.shape[1] - kept :]
    s_ref[...] = mm(q_ref[...], kt_ref[...])
    for at in chunks(0, q_ref.shape[0], STEP):
        scores = s_ref[at, :] + bias
        top = jnp.max(scores, -1, keepdims=True)
        expo = jnp.exp2(scores - top)
        e_ref[at, :] = expo.astype(BF16)
        peer_ref[at, :half] = jnp.broadcast_to(top, (STEP, half))
        peer_ref[at, half:] = jnp.broadcast_to(jnp.sum(expo, -1, keepdims=True), (STEP, half))
    top = jnp.maximum(stat_ref[:, :half], peer_ref[:, :half])
    own_part = jnp.exp2(stat_ref[:, :half] - top)
    peer_part = jnp.exp2(peer_ref[:, :half] - top)
    total = stat_ref[:, half:] * own_part + peer_ref[:, half:] * peer_part
    own_part, peer_part = own_part / total, peer_part / total
    for low in range(0, out_ref.shape[1], half):
        out_ref[:, low : low + half] = acc_ref[:, low : low + half] * own_part
    scale_ref[...] = peer_part


def peer_value_kernel(e_ref, v_ref, acc_ref, scale_ref, att_ref):
    summed = acc_ref[...] + mm(e_ref[...], v_ref[...]) * scale_ref[:, :1]
    att_ref[...] = unstack_heads(summed, att_ref.shape[0]).astype(BF16)


def out_project(att_ref, wo_refs, sum_ref):
    me = lax.axis_index("tensor")
    summed = mm(att_ref[me], wo_refs[0][...])
    for apart, wo_ref in enumerate(wo_refs[1:], 1):
        summed += mm(att_ref[me ^ apart], wo_ref[...])
    sum_ref[...] = summed


def sublayer(sum_ref, x_ref, norm_ref, at):
    return layer_norm(sum_ref[at, :] + norm_ref[0:1, :] + x_ref[at, :].astype(F32), norm_ref)


def second_kernel(
    bias_ref, att_ref, wo0, wo1, wo2, wo3, norm_ref, x_ref, picked_ref,
    wq_ref, wk_ref, wv_ref, bq_ref, bk_ref, bv_ref, kt_ref, v_ref, pkt_ref, pv_ref,
    second_ref, att_out_ref, s_ref, e_ref, sum_ref,
):
    count = x_ref.shape[0]
    out_project(att_ref, (wo0, wo1, wo2, wo3), sum_ref)
    for at in chunks(0, count, STEP):
        first = sublayer(sum_ref, x_ref, norm_ref, at)
        second_ref[at, :] = jnp.where(picked_ref[at, :1] == 1, first, x_ref[at, :])
    rows = second_ref[...]
    stacked = stack_queries(rows, wq_ref, bq_ref)
    own, cached = kt_ref.shape[1], kt_ref.shape[1] + pkt_ref.shape[1]
    s_ref[:, :own] = mm(stacked, kt_ref[...])
    s_ref[:, own:cached] = mm(stacked, pkt_ref[...])
    new_k = project(rows, wk_ref, bk_ref)
    new_v = project(rows, wv_ref, bv_ref)
    s_ref[:, cached:] = mm_t(stacked, new_k)
    bias = bias_ref[0:1, :]
    head_of = lax.broadcasted_iota(jnp.int32, att_out_ref.shape, 1) // HD
    merged = jnp.zeros(att_out_ref.shape, F32)
    for head, block in enumerate(chunks(0, stacked.shape[0], count)):
        sums = []
        for at in chunks(block.start, block.stop, STEP):
            s_old = s_ref[at, :cached] + bias
            s_new = s_ref[at, cached:]
            top = jnp.maximum(jnp.max(s_old, -1, keepdims=True), jnp.max(s_new, -1, keepdims=True))
            e_old = jnp.exp2(s_old - top)
            e_new = jnp.exp2(s_new - top)
            sums.append(jnp.sum(e_old, -1, keepdims=True) + jnp.sum(e_new, -1, keepdims=True))
            e_ref[at, :cached] = e_old.astype(BF16)
            e_ref[at, cached:] = e_new.astype(BF16)
        summed = (
            mm(e_ref[block, :own], v_ref[...])
            + mm(e_ref[block, own:cached], pv_ref[...])
            + mm(e_ref[block, cached:], new_v)
        ) / jnp.concatenate(sums, 0)
        merged = jnp.where(head_of == head, summed, merged)
    att_out_ref[...] = merged.astype(BF16)


def last_kernel(att_ref, wo0, wo1, wo2, wo3, norm_ref, x_ref, out_hbm, sum_ref, out_ref, sems):
    count = x_ref.shape[0]
    pieces = sems.shape[0]
    out_project(att_ref, (wo0, wo1, wo2, wo3), sum_ref)
    stores = []
    for piece, part in enumerate(chunks(0, count, count // pieces)):
        for at in chunks(part.start, part.stop, STEP):
            out_ref[at, :] = sublayer(sum_ref, x_ref, norm_ref, at)
        stores.append(pltpu.make_async_copy(out_ref.at[part], out_hbm.at[part], sems.at[piece]))
        stores[-1].start()
    for store in stores:
        store.wait()


def call(kernel, name, outs, *args, in_hbm=(), scratch=(), flops=1 << 10, limit=24, out_space=pltpu.VMEM):
    specs = [pl.BlockSpec(memory_space=pltpu.VMEM)] * len(args) + [pl.BlockSpec(memory_space=pltpu.HBM)] * len(in_hbm)
    return pl.pallas_call(
        kernel,
        name=name,
        out_shape=outs,
        in_specs=specs,
        out_specs=jax.tree.map(lambda _: pl.BlockSpec(memory_space=out_space), outs),
        scratch_shapes=scratch,
        compiler_params=pltpu.CompilerParams(vmem_limit_bytes=limit * MIB),
        cost_estimate=pl.CostEstimate(flops=flops, bytes_accessed=1 << 10, transcendentals=0),
    )(*args, *in_hbm)


def after(array, other):
    return lax.optimization_barrier((array, other))[0]


def moved(array, axis, apart):
    return lax.ppermute(array, axis, [(i, i ^ apart) for i in range(lax.axis_size(axis))])


def body(
    block, mask, cache_len, cache_k, cache_v, w_q, b_q, w_k, b_k, w_v, b_v, w_o, b_o, ln_gain, ln_shift
):
    rows = block[0]
    own_k, own_v = cache_k[0], cache_v[0]
    slab, width = own_k.shape
    count = rows.shape[0]
    stack = count * (width // HD)

    shape = jax.ShapeDtypeStruct
    dma = pltpu.SemaphoreType.DMA

    def sendable(array, name):
        return call(
            send_kernel, name, shape((slab - SHORTEST, width), BF16), in_hbm=(array,), scratch=[dma]
        )

    send_k = sendable(own_k, "send_k")
    send_v = sendable(after(own_v, send_k), "send_v")
    peer_k = moved(send_k, "group", 1)
    peer_v = moved(send_v, "group", 1)
    wo2 = moved(w_o, "tensor", 2)
    q_stack, acc, stats, picked, norm, bias, own_kt = call(
        own_kernel, "own",
        (shape((stack, width), BF16), shape((stack, width), F32), shape((stack, 256), F32),
         shape((count, 128), jnp.int32), shape((8, rows.shape[1]), F32),
         shape((8, 2 * slab - SHORTEST), F32), shape((width, slab), BF16)),
        cache_len.reshape(1, -1), mask, rows, w_q, w_k, w_v, b_q, b_k, b_v, own_k, own_v,
        b_o, ln_gain, ln_shift,
        scratch=[pltpu.VMEM((stack, slab + count), F32), pltpu.VMEM((stack, slab + count), BF16)],
    )
    wo1 = moved(after(w_o, acc), "tensor", 1)
    expo, acc, total, peer_kt = call(
        peer_score_kernel, "peer_score",
        (shape((stack, slab - SHORTEST), BF16), shape((stack, width), F32), shape((stack, 128), F32),
         shape((width, slab - SHORTEST), BF16)),
        bias, q_stack, peer_k, acc, stats, flops=1 << 33,
        scratch=[pltpu.VMEM((stack, slab - SHORTEST), F32), pltpu.VMEM((stack, 256), F32)],
    )
    wo3 = moved(after(wo2, expo), "tensor", 1)
    wo = (w_o, wo1, wo2, wo3)
    att = call(peer_value_kernel, "peer_value", shape((count, width), BF16), expo, peer_v, acc, total)
    att = lax.all_gather(att, "tensor")
    second, att = call(
        second_kernel, "second",
        (shape(rows.shape, BF16), shape((count, width), BF16)),
        bias, att, *wo, norm, rows, picked,
        w_q, w_k, w_v, b_q, b_k, b_v, own_kt, own_v, peer_kt, peer_v,
        scratch=[pltpu.VMEM((stack, 2 * slab), F32), pltpu.VMEM((stack, 2 * slab), BF16),
                 pltpu.VMEM(rows.shape, F32)],
    )
    att = lax.all_gather(att, "tensor")
    out = call(
        last_kernel, "last", shape(rows.shape, BF16), att, *wo, norm, second, out_space=pl.ANY,
        scratch=[pltpu.VMEM(rows.shape, F32), pltpu.VMEM(rows.shape, BF16), dma((4,))],
    )
    return out[None]


def solution(mesh):
    return jax.shard_map(
        body,
        mesh=mesh,
        in_specs=(
            P("group", None, None),
            P("group", None),
            P(),
            P("group", None, "tensor"),
            P("group", None, "tensor"),
            P(None, "tensor"),
            P("tensor"),
            P(None, "tensor"),
            P("tensor"),
            P(None, "tensor"),
            P("tensor"),
            P("tensor", None),
            P(),
            P(),
            P(),
        ),
        out_specs=P("group", None, None),
        check_vma=False,
    )
```

```python
import jax
import jax.numpy as jnp
from jax import lax
from jax.experimental import pallas as pl
from jax.experimental.pallas import tpu as pltpu
from jax.sharding import PartitionSpec as P

HD = 64
SHORTEST = 128
NEG = -1e30
EPS = 1e-05
F32 = jnp.float32
BF16 = jnp.bfloat16
MIB = 1 << 20
LOG2E = 1.4426950408889634
STEP = 16


def mm(left, right):
    return jnp.dot(left, right, preferred_element_type=F32)


def mm_t(left, right):
    return lax.dot_general(left, right, (((1,), (1,)), ((), ())), preferred_element_type=F32)


def project(rows, w_ref, b_ref):
    return (mm(rows, w_ref[...]) + b_ref[...].astype(F32)[None]).astype(BF16)


def stack_queries(rows, w_ref, b_ref):
    scaled = (
        (mm(rows, w_ref[...]) + b_ref[...].astype(F32)[None]) * F32(LOG2E * HD**-0.5)
    ).astype(BF16)
    head_of = lax.broadcasted_iota(jnp.int32, scaled.shape, 1) // HD
    heads = scaled.shape[1] // HD
    return jnp.concatenate(
        [jnp.where(head_of == head, scaled, jnp.zeros_like(scaled)) for head in range(heads)], 0
    )


def unstack_heads(stacked, rows):
    heads = stacked.shape[0] // rows
    head_of = lax.broadcasted_iota(jnp.int32, (rows, stacked.shape[1]), 1) // HD
    merged = stacked[:rows]
    for head in range(1, heads):
        merged = jnp.where(head_of == head, stacked[head * rows : (head + 1) * rows], merged)
    return merged


def read_length(len_ref):
    group = lax.axis_index("group")
    place = lax.broadcasted_iota(jnp.int32, len_ref.shape, 1)
    return jnp.sum(jnp.where(place == group, len_ref[...], 0), -1, keepdims=True)


def own_span(length, slab):
    even = lax.axis_index("group") % 2 == 0
    return jnp.where(even, 0, slab - length), jnp.where(even, length, slab)


def peer_span(length, kept):
    beyond = length - (kept + SHORTEST)
    even = lax.axis_index("group") % 2 == 0
    return jnp.where(even, 0, kept - beyond), jnp.where(even, beyond, kept)


def bias_row(count, span):
    low, high = span
    place = lax.broadcasted_iota(jnp.int32, (1, count), 1)
    return jnp.where((place >= low) & (place < high), F32(0), F32(NEG))


def column(row_ref):
    count = row_ref.shape[1]
    square = jnp.broadcast_to(row_ref[...], (count, count))
    across = lax.broadcasted_iota(jnp.int32, square.shape, 1)
    down = lax.broadcasted_iota(jnp.int32, square.shape, 0)
    return jnp.sum(jnp.where(across == down, square, 0), -1, keepdims=True)


def layer_norm(summed, norm_ref):
    centre = summed - jnp.mean(summed, -1, keepdims=True)
    spread = jnp.mean(centre * centre, -1, keepdims=True)
    return (centre * lax.rsqrt(spread + EPS) * norm_ref[1:2, :] + norm_ref[2:3, :]).astype(BF16)


def chunks(low, high, step):
    return [slice(start, start + step) for start in range(low, high, step)]


def own_kernel(
    len_ref, mask_ref, x_ref, wq_ref, wk_ref, wv_ref, bq_ref, bk_ref, bv_ref, k_ref, v_ref,
    bo_ref, gain_ref, shift_ref,
    q_ref, acc_ref, stat_ref, picked_ref, norm_ref, bias_ref, kt_ref, s_ref, e_ref,
):
    slab, count = k_ref.shape[0], x_ref.shape[0]
    rows = x_ref[...]
    stacked = stack_queries(rows, wq_ref, bq_ref)
    q_ref[...] = stacked
    kt_ref[...] = k_ref[...].T
    s_ref[:, :slab] = mm(stacked, kt_ref[...])
    new_k = project(rows, wk_ref, bk_ref)
    new_v = project(rows, wv_ref, bv_ref)
    s_ref[:, slab:] = mm_t(stacked, new_k)
    length = read_length(len_ref)
    own_bias = bias_row(slab, own_span(length, slab))
    bias_ref[:, :slab] = jnp.broadcast_to(own_bias, (bias_ref.shape[0], slab))
    kept = slab - SHORTEST
    bias_ref[:, slab:] = jnp.broadcast_to(
        bias_row(kept, peer_span(length, kept)), (bias_ref.shape[0], kept)
    )
    picked_ref[...] = jnp.broadcast_to(column(mask_ref), picked_ref.shape)
    for place, vector_ref in enumerate((bo_ref, gain_ref, shift_ref)):
        norm_ref[place : place + 1, :] = vector_ref[...].astype(F32)[None]
    bias = bias_ref[0:1, :slab]
    half = stat_ref.shape[1] // 2
    for block in chunks(0, stacked.shape[0], count):
        for at in chunks(block.start, block.stop, STEP):
            s_old = s_ref[at, :slab] + bias
            s_new = s_ref[at, slab:]
            top = jnp.maximum(jnp.max(s_old, -1, keepdims=True), jnp.max(s_new, -1, keepdims=True))
            e_old = jnp.exp2(s_old - top)
            e_new = jnp.exp2(s_new - top)
            total = jnp.sum(e_old, -1, keepdims=True) + jnp.sum(e_new, -1, keepdims=True)
            e_ref[at, :slab] = e_old.astype(BF16)
            e_ref[at, slab:] = e_new.astype(BF16)
            stat_ref[at, :half] = jnp.broadcast_to(top, (STEP, half))
            stat_ref[at, half:] = jnp.broadcast_to(total, (STEP, half))
        acc_ref[block, :] = mm(e_ref[block, :slab], v_ref[...]) + mm(e_ref[block, slab:], new_v)


def send_kernel(slab_hbm, out_ref, sem):
    kept = out_ref.shape[0]
    first = pl.multiple_of(
        jnp.where(lax.axis_index("group") % 2 == 0, slab_hbm.shape[0] - kept, 0), SHORTEST
    )
    load = pltpu.make_async_copy(slab_hbm.at[pl.ds(first, kept)], out_ref, sem)
    load.start()
    load.wait()


def peer_score_kernel(
    bias_ref, q_ref, k_ref, acc_ref, stat_ref, e_ref, out_ref, scale_ref, kt_ref, s_ref, peer_ref
):
    kept = k_ref.shape[0]
    half = stat_ref.shape[1] // 2
    kt_ref[...] = k_ref[...].T
    bias = bias_ref[0:1, bias_ref.shape[1] - kept :]
    s_ref[...] = mm(q_ref[...], kt_ref[...])
    for at in chunks(0, q_ref.shape[0], STEP):
        scores = s_ref[at, :] + bias
        top = jnp.max(scores, -1, keepdims=True)
        expo = jnp.exp2(scores - top)
        e_ref[at, :] = expo.astype(BF16)
        peer_ref[at, :half] = jnp.broadcast_to(top, (STEP, half))
        peer_ref[at, half:] = jnp.broadcast_to(jnp.sum(expo, -1, keepdims=True), (STEP, half))
    top = jnp.maximum(stat_ref[:, :half], peer_ref[:, :half])
    own_part = jnp.exp2(stat_ref[:, :half] - top)
    peer_part = jnp.exp2(peer_ref[:, :half] - top)
    total = stat_ref[:, half:] * own_part + peer_ref[:, half:] * peer_part
    own_part, peer_part = own_part / total, peer_part / total
    for low in range(0, out_ref.shape[1], half):
        out_ref[:, low : low + half] = acc_ref[:, low : low + half] * own_part
    scale_ref[...] = peer_part


def peer_value_kernel(e_ref, v_ref, acc_ref, scale_ref, att_ref):
    summed = acc_ref[...] + mm(e_ref[...], v_ref[...]) * scale_ref[:, :1]
    att_ref[...] = unstack_heads(summed, att_ref.shape[0]).astype(BF16)


def out_project(att_ref, wo_refs, sum_ref):
    me = lax.axis_index("tensor")
    summed = mm(att_ref[me], wo_refs[0][...])
    for apart, wo_ref in enumerate(wo_refs[1:], 1):
        summed += mm(att_ref[me ^ apart], wo_ref[...])
    sum_ref[...] = summed


def sublayer(sum_ref, x_ref, norm_ref, at):
    return layer_norm(sum_ref[at, :] + norm_ref[0:1, :] + x_ref[at, :].astype(F32), norm_ref)


def second_kernel(
    bias_ref, att_ref, wo0, wo1, wo2, wo3, norm_ref, x_ref, picked_ref,
    wq_ref, wk_ref, wv_ref, bq_ref, bk_ref, bv_ref, kt_ref, v_ref, pkt_ref, pv_ref,
    second_ref, att_out_ref, s_ref, e_ref, sum_ref,
):
    count = x_ref.shape[0]
    out_project(att_ref, (wo0, wo1, wo2, wo3), sum_ref)
    for at in chunks(0, count, STEP):
        first = sublayer(sum_ref, x_ref, norm_ref, at)
        second_ref[at, :] = jnp.where(picked_ref[at, :1] == 1, first, x_ref[at, :])
    rows = second_ref[...]
    stacked = stack_queries(rows, wq_ref, bq_ref)
    own, cached = kt_ref.shape[1], kt_ref.shape[1] + pkt_ref.shape[1]
    new_k = project(rows, wk_ref, bk_ref)
    new_v = project(rows, wv_ref, bv_ref)
    for block in chunks(0, stacked.shape[0], 256):
        s_ref[block, :own] = mm(stacked[block], kt_ref[...])
        s_ref[block, own:cached] = mm(stacked[block], pkt_ref[...])
        s_ref[block, cached:] = mm_t(stacked[block], new_k)
    bias = bias_ref[0:1, :]
    head_of = lax.broadcasted_iota(jnp.int32, att_out_ref.shape, 1) // HD
    merged = jnp.zeros(att_out_ref.shape, F32)
    for head, block in enumerate(chunks(0, stacked.shape[0], count)):
        sums = []
        for at in chunks(block.start, block.stop, STEP):
            s_old = s_ref[at, :cached] + bias
            s_new = s_ref[at, cached:]
            top = jnp.maximum(jnp.max(s_old, -1, keepdims=True), jnp.max(s_new, -1, keepdims=True))
            e_old = jnp.exp2(s_old - top)
            e_new = jnp.exp2(s_new - top)
            sums.append(jnp.sum(e_old, -1, keepdims=True) + jnp.sum(e_new, -1, keepdims=True))
            e_ref[at, :cached] = e_old.astype(BF16)
            e_ref[at, cached:] = e_new.astype(BF16)
        summed = (
            mm(e_ref[block, :own], v_ref[...])
            + mm(e_ref[block, own:cached], pv_ref[...])
            + mm(e_ref[block, cached:], new_v)
        ) / jnp.concatenate(sums, 0)
        merged = jnp.where(head_of == head, summed, merged)
    att_out_ref[...] = merged.astype(BF16)


def last_kernel(att_ref, wo0, wo1, wo2, wo3, norm_ref, x_ref, out_hbm, sum_ref, out_ref, sems):
    count = x_ref.shape[0]
    pieces = sems.shape[0]
    out_project(att_ref, (wo0, wo1, wo2, wo3), sum_ref)
    stores = []
    for piece, part in enumerate(chunks(0, count, count // pieces)):
        for at in chunks(part.start, part.stop, STEP):
            out_ref[at, :] = sublayer(sum_ref, x_ref, norm_ref, at)
        stores.append(pltpu.make_async_copy(out_ref.at[part], out_hbm.at[part], sems.at[piece]))
        stores[-1].start()
    for store in stores:
        store.wait()


def call(kernel, name, outs, *args, in_hbm=(), scratch=(), flops=1 << 10, limit=24, out_space=pltpu.VMEM):
    specs = [pl.BlockSpec(memory_space=pltpu.VMEM)] * len(args) + [pl.BlockSpec(memory_space=pltpu.HBM)] * len(in_hbm)
    return pl.pallas_call(
        kernel,
        name=name,
        out_shape=outs,
        in_specs=specs,
        out_specs=jax.tree.map(lambda _: pl.BlockSpec(memory_space=out_space), outs),
        scratch_shapes=scratch,
        compiler_params=pltpu.CompilerParams(vmem_limit_bytes=limit * MIB),
        cost_estimate=pl.CostEstimate(flops=flops, bytes_accessed=1 << 10, transcendentals=0),
    )(*args, *in_hbm)


def after(array, other):
    return lax.optimization_barrier((array, other))[0]


def moved(array, axis, apart):
    return lax.ppermute(array, axis, [(i, i ^ apart) for i in range(lax.axis_size(axis))])


def body(
    block, mask, cache_len, cache_k, cache_v, w_q, b_q, w_k, b_k, w_v, b_v, w_o, b_o, ln_gain, ln_shift
):
    rows = block[0]
    own_k, own_v = cache_k[0], cache_v[0]
    slab, width = own_k.shape
    count = rows.shape[0]
    stack = count * (width // HD)

    shape = jax.ShapeDtypeStruct
    dma = pltpu.SemaphoreType.DMA

    def sendable(array, name):
        return call(
            send_kernel, name, shape((slab - SHORTEST, width), BF16), in_hbm=(array,),
            scratch=[dma],
        )

    send_k = sendable(pltpu.with_memory_space_constraint(own_k, pltpu.HBM), "send_k")
    send_v = sendable(after(own_v, send_k), "send_v")
    peer_k = moved(send_k, "group", 1)
    peer_v = moved(send_v, "group", 1)
    wo2 = moved(w_o, "tensor", 2)
    q_stack, acc, stats, picked, norm, bias, own_kt = call(
        own_kernel, "own",
        (shape((stack, width), BF16), shape((stack, width), F32), shape((stack, 256), F32),
         shape((count, 128), jnp.int32), shape((8, rows.shape[1]), F32),
         shape((8, 2 * slab - SHORTEST), F32), shape((width, slab), BF16)),
        cache_len.reshape(1, -1), mask, rows, w_q, w_k, w_v, b_q, b_k, b_v, own_k, own_v,
        b_o, ln_gain, ln_shift,
        scratch=[pltpu.VMEM((stack, slab + count), F32), pltpu.VMEM((stack, slab + count), BF16)],
    )
    wo1 = moved(after(w_o, acc), "tensor", 1)
    expo, acc, total, peer_kt = call(
        peer_score_kernel, "peer_score",
        (shape((stack, slab - SHORTEST), BF16), shape((stack, width), F32), shape((stack, 128), F32),
         shape((width, slab - SHORTEST), BF16)),
        bias, q_stack, peer_k, acc, stats, flops=1 << 33,
        scratch=[pltpu.VMEM((stack, slab - SHORTEST), F32), pltpu.VMEM((stack, 256), F32)],
    )
    wo3 = moved(after(wo2, expo), "tensor", 1)
    wo = (w_o, wo1, wo2, wo3)
    att = call(peer_value_kernel, "peer_value", shape((count, width), BF16), expo, peer_v, acc, total)
    att = lax.all_gather(att, "tensor")
    second, att = call(
        second_kernel, "second",
        (shape(rows.shape, BF16), shape((count, width), BF16)),
        bias, att, *wo, norm, rows, picked,
        w_q, w_k, w_v, b_q, b_k, b_v, own_kt, own_v, peer_kt, peer_v,
        scratch=[pltpu.VMEM((stack, 2 * slab), F32), pltpu.VMEM((stack, 2 * slab), BF16),
                 pltpu.VMEM(rows.shape, F32)],
    )
    att = lax.all_gather(att, "tensor")
    out = call(
        last_kernel, "last", shape(rows.shape, BF16), att, *wo, norm, second, out_space=pl.ANY,
        scratch=[pltpu.VMEM(rows.shape, F32), pltpu.VMEM(rows.shape, BF16), dma((4,))],
    )
    return out[None]


def solution(mesh):
    return jax.shard_map(
        body,
        mesh=mesh,
        in_specs=(
            P("group", None, None),
            P("group", None),
            P(),
            P("group", None, "tensor"),
            P("group", None, "tensor"),
            P(None, "tensor"),
            P("tensor"),
            P(None, "tensor"),
            P("tensor"),
            P(None, "tensor"),
            P("tensor"),
            P("tensor", None),
            P(),
            P(),
            P(),
        ),
        out_specs=P("group", None, None),
        check_vma=False,
    )
```

```python
import jax
import jax.numpy as jnp
from jax import lax
from jax.experimental import pallas as pl
from jax.experimental.pallas import tpu as pltpu
from jax.sharding import PartitionSpec as P

HD = 64
SHORTEST = 128
NEG = -1e30
EPS = 1e-05
F32 = jnp.float32
BF16 = jnp.bfloat16
MIB = 1 << 20
LOG2E = 1.4426950408889634
STEP = 16


def mm(left, right):
    return jnp.dot(left, right, preferred_element_type=F32)


def mm_t(left, right):
    return lax.dot_general(left, right, (((1,), (1,)), ((), ())), preferred_element_type=F32)


def project(rows, w_ref, b_ref):
    return (mm(rows, w_ref[...]) + b_ref[...].astype(F32)[None]).astype(BF16)


def stack_queries(rows, w_ref, b_ref):
    scaled = (
        (mm(rows, w_ref[...]) + b_ref[...].astype(F32)[None]) * F32(LOG2E * HD**-0.5)
    ).astype(BF16)
    head_of = lax.broadcasted_iota(jnp.int32, scaled.shape, 1) // HD
    heads = scaled.shape[1] // HD
    return jnp.concatenate(
        [jnp.where(head_of == head, scaled, jnp.zeros_like(scaled)) for head in range(heads)], 0
    )


def unstack_heads(stacked, rows):
    heads = stacked.shape[0] // rows
    head_of = lax.broadcasted_iota(jnp.int32, (rows, stacked.shape[1]), 1) // HD
    merged = stacked[:rows]
    for head in range(1, heads):
        merged = jnp.where(head_of == head, stacked[head * rows : (head + 1) * rows], merged)
    return merged


def read_length(len_ref):
    group = lax.axis_index("group")
    place = lax.broadcasted_iota(jnp.int32, len_ref.shape, 1)
    return jnp.sum(jnp.where(place == group, len_ref[...], 0), -1, keepdims=True)


def own_span(length, slab):
    even = lax.axis_index("group") % 2 == 0
    return jnp.where(even, 0, slab - length), jnp.where(even, length, slab)


def peer_span(length, kept):
    beyond = length - (kept + SHORTEST)
    even = lax.axis_index("group") % 2 == 0
    return jnp.where(even, 0, kept - beyond), jnp.where(even, beyond, kept)


def bias_row(count, span):
    low, high = span
    place = lax.broadcasted_iota(jnp.int32, (1, count), 1)
    return jnp.where((place >= low) & (place < high), F32(0), F32(NEG))


def column(row_ref):
    count = row_ref.shape[1]
    square = jnp.broadcast_to(row_ref[...], (count, count))
    across = lax.broadcasted_iota(jnp.int32, square.shape, 1)
    down = lax.broadcasted_iota(jnp.int32, square.shape, 0)
    return jnp.sum(jnp.where(across == down, square, 0), -1, keepdims=True)


def layer_norm(summed, norm_ref):
    centre = summed - jnp.mean(summed, -1, keepdims=True)
    spread = jnp.mean(centre * centre, -1, keepdims=True)
    return (centre * lax.rsqrt(spread + EPS) * norm_ref[1:2, :] + norm_ref[2:3, :]).astype(BF16)


def chunks(low, high, step):
    return [slice(start, start + step) for start in range(low, high, step)]


def own_kernel(
    len_ref, mask_ref, x_ref, wq_ref, wk_ref, wv_ref, bq_ref, bk_ref, bv_ref, k_ref, v_ref,
    bo_ref, gain_ref, shift_ref,
    q_ref, acc_ref, stat_ref, picked_ref, norm_ref, bias_ref, kt_ref, s_ref, e_ref,
):
    slab, count = k_ref.shape[0], x_ref.shape[0]
    rows = x_ref[...]
    stacked = stack_queries(rows, wq_ref, bq_ref)
    q_ref[...] = stacked
    kt_ref[...] = k_ref[...].T
    s_ref[:, :slab] = mm(stacked, kt_ref[...])
    new_k = project(rows, wk_ref, bk_ref)
    new_v = project(rows, wv_ref, bv_ref)
    s_ref[:, slab:] = mm_t(stacked, new_k)
    length = read_length(len_ref)
    own_bias = bias_row(slab, own_span(length, slab))
    bias_ref[:, :slab] = jnp.broadcast_to(own_bias, (bias_ref.shape[0], slab))
    kept = slab - SHORTEST
    bias_ref[:, slab:] = jnp.broadcast_to(
        bias_row(kept, peer_span(length, kept)), (bias_ref.shape[0], kept)
    )
    picked_ref[...] = jnp.broadcast_to(column(mask_ref), picked_ref.shape)
    for place, vector_ref in enumerate((bo_ref, gain_ref, shift_ref)):
        norm_ref[place : place + 1, :] = vector_ref[...].astype(F32)[None]
    bias = bias_ref[0:1, :slab]
    half = stat_ref.shape[1] // 2
    for block in chunks(0, stacked.shape[0], count):
        for at in chunks(block.start, block.stop, STEP):
            s_old = s_ref[at, :slab] + bias
            s_new = s_ref[at, slab:]
            top = jnp.maximum(jnp.max(s_old, -1, keepdims=True), jnp.max(s_new, -1, keepdims=True))
            e_old = jnp.exp2(s_old - top)
            e_new = jnp.exp2(s_new - top)
            total = jnp.sum(e_old, -1, keepdims=True) + jnp.sum(e_new, -1, keepdims=True)
            e_ref[at, :slab] = e_old.astype(BF16)
            e_ref[at, slab:] = e_new.astype(BF16)
            stat_ref[at, :half] = jnp.broadcast_to(top, (STEP, half))
            stat_ref[at, half:] = jnp.broadcast_to(total, (STEP, half))
        acc_ref[block, :] = mm(e_ref[block, :slab], v_ref[...]) + mm(e_ref[block, slab:], new_v)


def send_kernel(slab_hbm, out_ref, sem):
    kept = out_ref.shape[0]
    first = pl.multiple_of(
        jnp.where(lax.axis_index("group") % 2 == 0, slab_hbm.shape[0] - kept, 0), SHORTEST
    )
    load = pltpu.make_async_copy(slab_hbm.at[pl.ds(first, kept)], out_ref, sem)
    load.start()
    load.wait()


def peer_score_kernel(
    bias_ref, q_ref, k_ref, acc_ref, stat_ref, e_ref, out_ref, scale_ref, kt_ref, s_ref, peer_ref
):
    kept = kt_ref.shape[1]
    half = stat_ref.shape[1] // 2
    first = pl.multiple_of(
        jnp.where(lax.axis_index("group") % 2 == 0, 0, k_ref.shape[0] - kept), SHORTEST
    )
    kt_ref[...] = k_ref[pl.ds(first, kept), :].T
    bias = bias_ref[0:1, bias_ref.shape[1] - kept :]
    s_ref[...] = mm(q_ref[...], kt_ref[...])
    for at in chunks(0, q_ref.shape[0], STEP):
        scores = s_ref[at, :] + bias
        top = jnp.max(scores, -1, keepdims=True)
        expo = jnp.exp2(scores - top)
        e_ref[at, :] = expo.astype(BF16)
        peer_ref[at, :half] = jnp.broadcast_to(top, (STEP, half))
        peer_ref[at, half:] = jnp.broadcast_to(jnp.sum(expo, -1, keepdims=True), (STEP, half))
    top = jnp.maximum(stat_ref[:, :half], peer_ref[:, :half])
    own_part = jnp.exp2(stat_ref[:, :half] - top)
    peer_part = jnp.exp2(peer_ref[:, :half] - top)
    total = stat_ref[:, half:] * own_part + peer_ref[:, half:] * peer_part
    own_part, peer_part = own_part / total, peer_part / total
    for low in range(0, out_ref.shape[1], half):
        out_ref[:, low : low + half] = acc_ref[:, low : low + half] * own_part
    scale_ref[...] = peer_part


def peer_value_kernel(e_ref, v_ref, acc_ref, scale_ref, att_ref):
    summed = acc_ref[...] + mm(e_ref[...], v_ref[...]) * scale_ref[:, :1]
    att_ref[...] = unstack_heads(summed, att_ref.shape[0]).astype(BF16)


def out_project(att_ref, wo_refs, sum_ref):
    me = lax.axis_index("tensor")
    summed = mm(att_ref[me], wo_refs[0][...])
    for apart, wo_ref in enumerate(wo_refs[1:], 1):
        summed += mm(att_ref[me ^ apart], wo_ref[...])
    sum_ref[...] = summed


def sublayer(sum_ref, x_ref, norm_ref, at):
    return layer_norm(sum_ref[at, :] + norm_ref[0:1, :] + x_ref[at, :].astype(F32), norm_ref)


def second_kernel(
    bias_ref, att_ref, wo0, wo1, wo2, wo3, norm_ref, x_ref, picked_ref,
    wq_ref, wk_ref, wv_ref, bq_ref, bk_ref, bv_ref, kt_ref, v_ref, pkt_ref, pv_ref,
    second_ref, att_out_ref, s_ref, e_ref, sum_ref,
):
    count = x_ref.shape[0]
    out_project(att_ref, (wo0, wo1, wo2, wo3), sum_ref)
    for at in chunks(0, count, STEP):
        first = sublayer(sum_ref, x_ref, norm_ref, at)
        second_ref[at, :] = jnp.where(picked_ref[at, :1] == 1, first, x_ref[at, :])
    rows = second_ref[...]
    stacked = stack_queries(rows, wq_ref, bq_ref)
    own, cached = kt_ref.shape[1], kt_ref.shape[1] + pkt_ref.shape[1]
    new_k = project(rows, wk_ref, bk_ref)
    new_v = project(rows, wv_ref, bv_ref)
    for block in chunks(0, stacked.shape[0], 256):
        s_ref[block, :own] = mm(stacked[block], kt_ref[...])
        s_ref[block, own:cached] = mm(stacked[block], pkt_ref[...])
        s_ref[block, cached:] = mm_t(stacked[block], new_k)
    bias = bias_ref[0:1, :]
    head_of = lax.broadcasted_iota(jnp.int32, att_out_ref.shape, 1) // HD
    merged = jnp.zeros(att_out_ref.shape, F32)
    for head, block in enumerate(chunks(0, stacked.shape[0], count)):
        sums = []
        for at in chunks(block.start, block.stop, STEP):
            s_old = s_ref[at, :cached] + bias
            s_new = s_ref[at, cached:]
            top = jnp.maximum(jnp.max(s_old, -1, keepdims=True), jnp.max(s_new, -1, keepdims=True))
            e_old = jnp.exp2(s_old - top)
            e_new = jnp.exp2(s_new - top)
            sums.append(jnp.sum(e_old, -1, keepdims=True) + jnp.sum(e_new, -1, keepdims=True))
            e_ref[at, :cached] = e_old.astype(BF16)
            e_ref[at, cached:] = e_new.astype(BF16)
        summed = (
            mm(e_ref[block, :own], v_ref[...])
            + mm(e_ref[block, own:cached], pv_ref[...])
            + mm(e_ref[block, cached:], new_v)
        ) / jnp.concatenate(sums, 0)
        merged = jnp.where(head_of == head, summed, merged)
    att_out_ref[...] = merged.astype(BF16)


def last_kernel(att_ref, wo0, wo1, wo2, wo3, norm_ref, x_ref, out_hbm, sum_ref, out_ref, sems):
    count = x_ref.shape[0]
    pieces = sems.shape[0]
    out_project(att_ref, (wo0, wo1, wo2, wo3), sum_ref)
    stores = []
    for piece, part in enumerate(chunks(0, count, count // pieces)):
        for at in chunks(part.start, part.stop, STEP):
            out_ref[at, :] = sublayer(sum_ref, x_ref, norm_ref, at)
        stores.append(pltpu.make_async_copy(out_ref.at[part], out_hbm.at[part], sems.at[piece]))
        stores[-1].start()
    for store in stores:
        store.wait()


def call(kernel, name, outs, *args, in_hbm=(), scratch=(), flops=1 << 10, limit=24, out_space=pltpu.VMEM):
    specs = [pl.BlockSpec(memory_space=pltpu.VMEM)] * len(args) + [pl.BlockSpec(memory_space=pltpu.HBM)] * len(in_hbm)
    return pl.pallas_call(
        kernel,
        name=name,
        out_shape=outs,
        in_specs=specs,
        out_specs=jax.tree.map(lambda _: pl.BlockSpec(memory_space=out_space), outs),
        scratch_shapes=scratch,
        compiler_params=pltpu.CompilerParams(vmem_limit_bytes=limit * MIB),
        cost_estimate=pl.CostEstimate(flops=flops, bytes_accessed=1 << 10, transcendentals=0),
    )(*args, *in_hbm)


def after(array, other):
    return lax.optimization_barrier((array, other))[0]


def moved(array, axis, apart):
    return lax.ppermute(array, axis, [(i, i ^ apart) for i in range(lax.axis_size(axis))])


def body(
    block, mask, cache_len, cache_k, cache_v, w_q, b_q, w_k, b_k, w_v, b_v, w_o, b_o, ln_gain, ln_shift
):
    rows = block[0]
    own_k, own_v = cache_k[0], cache_v[0]
    slab, width = own_k.shape
    count = rows.shape[0]
    stack = count * (width // HD)

    shape = jax.ShapeDtypeStruct
    dma = pltpu.SemaphoreType.DMA

    def sendable(array, name):
        return call(
            send_kernel, name, shape((slab - SHORTEST, width), BF16), in_hbm=(array,),
            scratch=[dma],
        )

    send_v = sendable(own_v, "send_v")
    peer_k = moved(own_k, "group", 1)
    peer_v = moved(send_v, "group", 1)
    wo2 = moved(w_o, "tensor", 2)
    q_stack, acc, stats, picked, norm, bias, own_kt = call(
        own_kernel, "own",
        (shape((stack, width), BF16), shape((stack, width), F32), shape((stack, 256), F32),
         shape((count, 128), jnp.int32), shape((8, rows.shape[1]), F32),
         shape((8, 2 * slab - SHORTEST), F32), shape((width, slab), BF16)),
        cache_len.reshape(1, -1), mask, rows, w_q, w_k, w_v, b_q, b_k, b_v, own_k, own_v,
        b_o, ln_gain, ln_shift,
        scratch=[pltpu.VMEM((stack, slab + count), F32), pltpu.VMEM((stack, slab + count), BF16)],
    )
    wo1 = moved(after(w_o, acc), "tensor", 1)
    expo, acc, total, peer_kt = call(
        peer_score_kernel, "peer_score",
        (shape((stack, slab - SHORTEST), BF16), shape((stack, width), F32), shape((stack, 128), F32),
         shape((width, slab - SHORTEST), BF16)),
        bias, q_stack, peer_k, acc, stats, flops=1 << 33,
        scratch=[pltpu.VMEM((stack, slab - SHORTEST), F32), pltpu.VMEM((stack, 256), F32)],
    )
    wo3 = moved(after(wo2, expo), "tensor", 1)
    wo = (w_o, wo1, wo2, wo3)
    att = call(peer_value_kernel, "peer_value", shape((count, width), BF16), expo, peer_v, acc, total)
    att = lax.all_gather(att, "tensor")
    second, att = call(
        second_kernel, "second",
        (shape(rows.shape, BF16), shape((count, width), BF16)),
        bias, att, *wo, norm, rows, picked,
        w_q, w_k, w_v, b_q, b_k, b_v, own_kt, own_v, peer_kt, peer_v,
        scratch=[pltpu.VMEM((stack, 2 * slab), F32), pltpu.VMEM((stack, 2 * slab), BF16),
                 pltpu.VMEM(rows.shape, F32)],
    )
    att = lax.all_gather(att, "tensor")
    out = call(
        last_kernel, "last", shape(rows.shape, BF16), att, *wo, norm, second, out_space=pl.ANY,
        scratch=[pltpu.VMEM(rows.shape, F32), pltpu.VMEM(rows.shape, BF16), dma((4,))],
    )
    return out[None]


def solution(mesh):
    return jax.shard_map(
        body,
        mesh=mesh,
        in_specs=(
            P("group", None, None),
            P("group", None),
            P(),
            P("group", None, "tensor"),
            P("group", None, "tensor"),
            P(None, "tensor"),
            P("tensor"),
            P(None, "tensor"),
            P("tensor"),
            P(None, "tensor"),
            P("tensor"),
            P("tensor", None),
            P(),
            P(),
            P(),
        ),
        out_specs=P("group", None, None),
        check_vma=False,
    )
```
